32 devices in a mesh: groups: 2 (over y), seq: 8 (over z, x), enc: 2 (over core).
Axes of the slice: x: 2, y: 2, z: 4, core: 2. Of those that a mesh axis runs over, the one named last changes fastest.
Arguments:
- self_queries: bfloat16 [2, 256, 4096], P('enc', ('groups', 'seq')), parts along dimension 1, may hold values from -32 to 32
- self_keys: bfloat16 [2, 256, 4096], P('enc', ('groups', 'seq')), parts along dimension 1, may hold values from -32 to 32
- self_values: bfloat16 [2, 256, 4096], P('enc', ('groups', 'seq')), parts along dimension 1, may hold values from -6 to 6
- text_queries: bfloat16 [2, 256, 4096], P('enc', ('groups', 'seq')), parts along dimension 1, may hold values from -32 to 32
- text_kv: bfloat16 [2, 2, 1024, 4096], P('enc', None, ('groups', 'seq')), parts along dimension 2, may hold values from -32 to 32
- text_len: int32 [4], P('groups'), parts along dimension 0, may hold values from 16 to 512
Outputs:
- self_mixed: bfloat16 [2, 256, 4096], P('enc', ('groups', 'seq')), parts along dimension 1
- text_mixed: bfloat16 [2, 256, 4096], P('enc', ('groups', 'seq')), parts along dimension 1
The draws below stay inside these ranges and needn't reach their ends.
There are 2 independent parts, one for each index of `groups`. The reference program is written for one: setup_inputs(seed, part) draws one part's arguments, and reference() takes and returns one part's arrays. A program takes and returns all parts, laid end to end along the dimension named above; each array names one. Nothing has to cross between parts.
Inputs may be any that keep to these rules, and one draw needn't show every extreme that they name: `text_len`: entry 0 is the prompt's length, entry 1 the negative prompt's; text rows at or past a length are padding.
All inputs are finite; a program needn't handle non-finite values.
Results may differ from the reference program's by a relative error of at most 0.0034.
Values may be sent and summed in bfloat16 or wider, within the bound.
No kernel may reach another device: no remote copies, remote signals or barrier semaphores. Data moves between devices by JAX's collectives and lax.ppermute only.
A program may use at most 64 MiB of HBM per device.

```python
import math
import jax
import jax.numpy as jnp
from jax import lax

HEADS = 32
HEAD_DIM = 128
TEXT = 512
SEQ = 128
CHANNELS = 4096


def row_scaled(key, shape, scale):
    base = scale * jax.random.truncated_normal(jax.random.fold_in(key, 1), -4.0, 4.0, shape, jnp.float32)
    return base


def draw_self_queries(key, part):
    queries = row_scaled(jax.random.fold_in(key, 11), (2, SEQ, CHANNELS), 1.6)
    return queries.astype(jnp.bfloat16)


def draw_self_keys(key, part):
    key_table = row_scaled(jax.random.fold_in(key, 12), (2, SEQ, CHANNELS), 1.6)
    return key_table.astype(jnp.bfloat16)


def draw_text_queries(key, part):
    queries = row_scaled(jax.random.fold_in(key, 13), (2, SEQ, CHANNELS), 1.6)
    return queries.astype(jnp.bfloat16)


def draw_text_kv(key, part):
    key_table = row_scaled(jax.random.fold_in(key, 14), (2, TEXT, CHANNELS), 1.6)
    value_table = jax.random.truncated_normal(jax.random.fold_in(key, 15), -4.0, 4.0, (2, TEXT, CHANNELS), jnp.float32)
    return jnp.stack([key_table, value_table], axis=1).astype(jnp.bfloat16)


def block_levels(stream_key, dims, cuts, low, largest):
    loudness, own = 1.0, jax.random.fold_in(stream_key, 6)
    for position, blocks in cuts:
        steps = jnp.exp(jax.random.uniform(jax.random.fold_in(own, position), (blocks,), jnp.float32, low / len(cuts), largest / len(cuts)))
        loudness = loudness * jnp.repeat(steps, dims[position] // blocks).reshape([-1 if axis == position else 1 for axis in range(len(dims))])
    return loudness


def gaussian(stream_key, dims, scale, limit, shards=(), held_as=jnp.bfloat16):
    entries = scale * jax.random.normal(stream_key, dims, jnp.float32)
    if shards:
        entries = entries * block_levels(stream_key, dims, shards, -0.22, 0.18)
    return jnp.clip(entries, -limit, limit).astype(held_as)


def setup_inputs(seed: int = 0, part: int = 0) -> dict:
    key_list = jax.random.split(jax.random.key(seed), 7)
    own_keys = jax.random.split(jax.random.fold_in(key_list[6], part), 7)
    self_queries = draw_self_queries(jax.random.fold_in(jax.random.fold_in(key_list[6], part), 71), part)
    self_keys = draw_self_keys(jax.random.fold_in(jax.random.fold_in(key_list[6], part), 71), part)
    self_values = gaussian(own_keys[2], (2, SEQ, CHANNELS), 1.0, 6.0, ((0, 2), (1, 8)))
    text_queries = draw_text_queries(jax.random.fold_in(jax.random.fold_in(key_list[6], part), 71), part)
    text_kv = draw_text_kv(jax.random.fold_in(jax.random.fold_in(key_list[6], part), 71), part)
    text_len = jax.random.randint(own_keys[5], (2,), 16, TEXT + 1).astype(jnp.int32)
    return dict(self_queries=self_queries, self_keys=self_keys, self_values=self_values, text_queries=text_queries, text_kv=text_kv, text_len=text_len)


def head_attention(query_rows, key_rows, value_rows, live_mask):
    scores = jnp.dot(query_rows, key_rows.T, preferred_element_type=jnp.float32) / math.sqrt(HEAD_DIM)
    scores = jnp.where(live_mask[None, :], scores, -1e+30)
    shifted = jnp.where(live_mask[None, :], jnp.exp(scores - lax.optimization_barrier(jnp.max(scores, axis=1, keepdims=True))), 0.0)
    blended = jnp.dot(shifted.astype(jnp.bfloat16), value_rows, preferred_element_type=jnp.float32)
    return (blended / lax.optimization_barrier(jnp.sum(shifted, axis=1, keepdims=True))).astype(jnp.bfloat16)

def by_heads(tensor):
    return tensor.reshape(tensor.shape[0], HEADS, HEAD_DIM).transpose(1, 0, 2)

def from_heads(tensor):
    return tensor.transpose(1, 0, 2).reshape(tensor.shape[1], HEADS * HEAD_DIM)

def attend_all(queries, key_rows, value_rows, live_mask):

    def one_head(triple):
        return head_attention(triple[0], triple[1], triple[2], live_mask)
    return from_heads(lax.map(one_head, (by_heads(queries), by_heads(key_rows), by_heads(value_rows))))

def reference(self_queries, self_keys, self_values, text_queries, text_kv, text_len):
    self_list = []
    text_list = []
    positions = jnp.arange(TEXT, dtype=jnp.int32)
    every_key = jnp.ones((SEQ,), jnp.bool_)
    for branch in range(2):
        self_list.append(attend_all(self_queries[branch], self_keys[branch], self_values[branch], every_key))
        live_mask = positions < text_len[branch]
        text_list.append(attend_all(text_queries[branch], text_kv[branch, 0], text_kv[branch, 1], live_mask))
    return (jnp.stack(self_list), jnp.stack(text_list))
```

```python
import functools
import math

import jax
import jax.numpy as jnp
from jax import lax
from jax.experimental import pallas as pl
from jax.experimental.pallas import tpu as pltpu
from jax.sharding import PartitionSpec as P

HEADS = 32
HEAD_DIM = 128
LANES = 128


def absorb(run_state, queries, key_rows, value_rows, live_mask):
    running_max, row_total, weighted_sum = run_state
    scores = jnp.einsum(
        "qpd,kpd->pqk", queries, key_rows, preferred_element_type=jnp.float32
    ) / math.sqrt(HEAD_DIM)
    scores = jnp.where(live_mask[None, None, :], scores, -1e30)
    new_max = jnp.maximum(running_max, jnp.max(scores, axis=2))
    weights = jnp.where(live_mask[None, None, :], jnp.exp(scores - new_max[:, :, None]), 0.0)
    factor = jnp.exp(running_max - new_max)
    row_total = row_total * factor + jnp.sum(weights, axis=2)
    weighted_sum = weighted_sum * factor[:, :, None] + jnp.einsum(
        "pqk,kpd->pqd", weights.astype(jnp.bfloat16), value_rows, preferred_element_type=jnp.float32
    )
    return (new_max, row_total, weighted_sum)


def empty_state(head_count, query_count):
    return (
        jnp.full((head_count, query_count), -1e30, jnp.float32),
        jnp.zeros((head_count, query_count), jnp.float32),
        jnp.zeros((head_count, query_count, HEAD_DIM), jnp.float32),
    )


def finish(run_state):
    running_max, row_total, weighted_sum = run_state
    return (weighted_sum / row_total[:, :, None]).transpose(1, 0, 2).astype(jnp.bfloat16)


def block_attention(queries, key_rows, value_rows, live_mask):
    query_total, heads_here, head_width = queries.shape
    key_total = key_rows.shape[0]
    key_block = 1024 if key_total % 1024 == 0 else key_total
    query_block = 512 if query_total % 512 == 0 else query_total
    key_blocks = key_rows.reshape(key_total // key_block, key_block, heads_here, head_width)
    value_blocks = value_rows.reshape(key_total // key_block, key_block, heads_here, head_width)
    live_blocks = live_mask.reshape(key_total // key_block, key_block)

    def one_block(query_piece):

        def absorb_block(run_state, pieces):
            return (absorb(run_state, query_piece, pieces[0], pieces[1], pieces[2]), None)

        final_state, unused = lax.scan(
            absorb_block,
            empty_state(heads_here, query_block),
            (key_blocks, value_blocks, live_blocks),
        )
        return finish(final_state)

    blended = lax.map(
        one_block, queries.reshape(query_total // query_block, query_block, heads_here, head_width)
    )
    return blended.reshape(query_total, heads_here, head_width)


def general_shards(self_queries, self_keys, self_values, text_queries, text_kv, text_len):
    token_rows = self_queries.shape[1]
    channel_count = self_queries.shape[2]
    seq_count = lax.axis_size("seq")
    quarter_count = max(seq_count // HEADS, 1)
    heads_here = max(HEADS // seq_count, 1)
    group_count = HEADS // heads_here
    head_span = heads_here * HEAD_DIM
    share_rows = token_rows // quarter_count
    query_total = share_rows * seq_count
    branch = lax.axis_index("enc")
    length = lax.dynamic_index_in_dim(text_len, branch, 0, keepdims=False)

    def head_view(tensor):
        return tensor.reshape(1, share_rows, seq_count, head_span)

    def repeated(tensor):
        spread = jnp.broadcast_to(
            tensor.reshape(1, token_rows, 1, group_count, head_span),
            (1, token_rows, quarter_count, group_count, head_span),
        )
        return spread.reshape(1, token_rows, seq_count, head_span)

    head_queries, head_keys, head_values = (
        lax.all_to_all(head_view(self_queries), "seq", split_axis=2, concat_axis=1, tiled=True),
        lax.all_to_all(repeated(self_keys), "seq", split_axis=2, concat_axis=1, tiled=True),
        lax.all_to_all(repeated(self_values), "seq", split_axis=2, concat_axis=1, tiled=True),
    )
    key_rows = head_keys.reshape(-1, heads_here, HEAD_DIM)
    value_rows = head_values.reshape(-1, heads_here, HEAD_DIM)
    query_rows = head_queries.reshape(query_total, heads_here, HEAD_DIM)
    every_key = jnp.ones((key_rows.shape[0],), jnp.bool_)
    self_heads = block_attention(query_rows, key_rows, value_rows, every_key)
    head_text_queries = lax.all_to_all(
        head_view(text_queries), "seq", split_axis=2, concat_axis=1, tiled=True
    )
    context_rows = text_kv.shape[2]
    spread = jnp.broadcast_to(
        text_kv.reshape(1, 2, context_rows, 1, group_count, head_span),
        (1, 2, context_rows, quarter_count, group_count, head_span),
    )
    head_context = lax.all_to_all(
        spread.reshape(1, 2, context_rows, seq_count, head_span),
        "seq",
        split_axis=3,
        concat_axis=2,
        tiled=True,
    )
    text_total = head_context.shape[2]
    context_keys = head_context[0, 0].reshape(text_total, heads_here, HEAD_DIM)
    context_values = head_context[0, 1].reshape(text_total, heads_here, HEAD_DIM)
    live_mask = jnp.arange(text_total, dtype=jnp.int32) < length
    text_heads = block_attention(
        head_text_queries.reshape(query_total, heads_here, HEAD_DIM),
        context_keys,
        context_values,
        live_mask,
    )
    self_view = self_heads.reshape(1, seq_count, share_rows, 1, head_span)
    text_view = text_heads.reshape(1, seq_count, share_rows, 1, head_span)
    self_back, text_back = (
        lax.all_to_all(self_view, "seq", split_axis=1, concat_axis=3, tiled=True),
        lax.all_to_all(text_view, "seq", split_axis=1, concat_axis=3, tiled=True),
    )
    self_mixed = self_back.reshape(1, token_rows, channel_count)
    text_mixed = text_back.reshape(1, token_rows, channel_count)
    return (self_mixed, text_mixed)


VMEM_SPEC = pl.BlockSpec(memory_space=pltpu.VMEM)
HBM_SPEC = pl.BlockSpec(memory_space=pl.ANY)
SMEM_SPEC = pl.BlockSpec(memory_space=pltpu.SMEM)


def columns(index, width):
    return pl.ds(pl.multiple_of(index * width, width), width)


def pack_text_kernel(half, text_ref, *refs):
    out_refs, sems = refs[:half], refs[half]
    me = lax.axis_index("seq")
    width = out_refs[0].shape[2]
    copies = []
    for step in range(half):
        group = lax.rem(me ^ step, half)
        copies.append(
            pltpu.make_async_copy(
                text_ref.at[0, :, :, columns(group, width)], out_refs[step], sems.at[step]
            )
        )
    for copy in copies:
        copy.start()
    for copy in copies:
        copy.wait()


def pack_rows_kernel(count, self_span, text_span, q_ref, k_ref, v_ref, t_ref, *refs):
    out_refs, sems = refs[:count], refs[count]
    me = lax.axis_index("seq")
    copies = []
    for step in range(count):
        other = me ^ step
        for place, source in enumerate((q_ref, k_ref, v_ref)):
            copies.append(
                pltpu.make_async_copy(
                    source.at[0, :, columns(other, self_span)],
                    out_refs[step].at[:, pl.ds(place * self_span, self_span)],
                    sems.at[step, place],
                )
            )
        copies.append(
            pltpu.make_async_copy(
                t_ref.at[0, :, columns(lax.rem(other, count // 2), text_span)],
                out_refs[step].at[:, pl.ds(3 * self_span, text_span)],
                sems.at[step, 3],
            )
        )
    for copy in copies:
        copy.start()
    for copy in copies:
        copy.wait()


def matmul_nt(a, b):
    return lax.dot_general(a, b, (((1,), (1,)), ((), ())), preferred_element_type=jnp.float32)


def attend_kernel(count, self_heads, text_heads, length_ref, *refs):
    half = count // 2
    text_refs, row_refs = refs[:half][::-1], refs[half : half + count][::-1]
    out_refs = refs[half + count :]
    rows = row_refs[0].shape[0]
    self_span, text_span = self_heads * HEAD_DIM, text_heads * HEAD_DIM
    context_rows = text_refs[0].shape[1]
    total = rows * count
    scale = 1.0 / math.sqrt(HEAD_DIM)
    me = lax.axis_index("seq")
    length = length_ref[lax.axis_index("enc")]

    def gathered(start):
        return jnp.concatenate([ref[:, pl.ds(start, HEAD_DIM)] for ref in row_refs], axis=0)

    def put(start, values):
        for step in range(count):
            out_refs[step][:, pl.ds(start, values.shape[1])] = values[step * rows : (step + 1) * rows]

    for head in range(self_heads):
        at = head * HEAD_DIM
        queries, keys, values = (gathered(place * self_span + at) for place in range(3))
        scores = matmul_nt(queries, keys) * scale
        top = jnp.max(scores, axis=1, keepdims=True)
        weights = jnp.exp(scores - top)
        row_sum = jnp.sum(weights, axis=1, keepdims=True)
        mixed = jnp.dot(weights.astype(jnp.bfloat16), values, preferred_element_type=jnp.float32)
        put(at, (mixed / row_sum).astype(jnp.bfloat16))

    spots = lax.broadcasted_iota(jnp.int32, (1, half * context_rows), 1)
    block = lax.div(spots, context_rows)
    position = (me ^ block) * context_rows + (spots - block * context_rows)
    dead_bias = jnp.where(position < length, 0.0, -1e30)
    any_live = length > lax.div(me, half) * (half * context_rows)
    lane = lax.broadcasted_iota(jnp.int32, (total, LANES), 1)
    stats = jnp.zeros((total, LANES), jnp.float32)
    for head in range(text_heads):
        at = head * HEAD_DIM
        queries = gathered(3 * self_span + at)
        keys = jnp.concatenate([ref[0, :, pl.ds(at, HEAD_DIM)] for ref in text_refs], axis=0)
        values = jnp.concatenate([ref[1, :, pl.ds(at, HEAD_DIM)] for ref in text_refs], axis=0)
        scores = matmul_nt(queries, keys) * scale + dead_bias
        top = jnp.max(scores, axis=1, keepdims=True)
        weights = jnp.exp(scores - top)
        row_sum = jnp.sum(weights, axis=1, keepdims=True)
        mixed = jnp.dot(weights.astype(jnp.bfloat16), values, preferred_element_type=jnp.float32)
        put(self_span + at, (mixed / row_sum).astype(jnp.bfloat16))
        live_sum = jnp.where(any_live, row_sum, 0.0)
        stats = jnp.where(lane == head, top, stats)
        stats = jnp.where(lane == text_heads + head, live_sum, stats)
    high = stats.astype(jnp.bfloat16).astype(jnp.float32)
    rest = stats - high
    middle = rest.astype(jnp.bfloat16).astype(jnp.float32)
    low = rest - middle
    stride = 2 * text_heads
    pieces = high + pltpu.roll(middle, stride, 1) + pltpu.roll(low, 2 * stride, 1)
    put(self_span + text_span, pieces.astype(jnp.bfloat16))


def combine_kernel(count, self_heads, text_heads, *refs):
    half = count // 2
    in_refs, (self_ref, text_ref) = refs[:count][::-1], refs[count:]
    self_span, text_span = self_heads * HEAD_DIM, text_heads * HEAD_DIM
    me = lax.axis_index("seq")
    stride = 2 * text_heads

    def read_stats(ref):
        pieces = ref[:, pl.ds(self_span + text_span, LANES)].astype(jnp.float32)
        stats = pieces + (
            pltpu.roll(pieces, LANES - stride, 1) + pltpu.roll(pieces, LANES - 2 * stride, 1)
        )
        return stats, pltpu.roll(stats, LANES - text_heads, 1)

    for step in range(count):
        self_ref[0, :, columns(me ^ step, self_span)] = in_refs[step][:, pl.ds(0, self_span)]
    for step in range(half):
        near, far = in_refs[step], in_refs[step ^ half]
        near_top, near_sum = read_stats(near)
        far_top, far_sum = read_stats(far)
        top = jnp.maximum(near_top, far_top)
        near_part = near_sum * jnp.exp(near_top - top)
        far_part = far_sum * jnp.exp(far_top - top)
        both = near_part + far_part
        near_share, far_share = near_part / both, far_part / both
        group = lax.rem(me ^ step, half)
        for head in range(text_heads):
            at = self_span + head * HEAD_DIM
            mixed = near[:, pl.ds(at, HEAD_DIM)].astype(jnp.float32) * near_share[:, head : head + 1]
            mixed += far[:, pl.ds(at, HEAD_DIM)].astype(jnp.float32) * far_share[:, head : head + 1]
            text_ref[0, :, columns(group * text_heads + head, HEAD_DIM)] = mixed.astype(jnp.bfloat16)


def halves_shards(self_queries, self_keys, self_values, text_queries, text_kv, text_len):
    count = lax.axis_size("seq")
    half = count // 2
    rows, channels = self_queries.shape[1], self_queries.shape[2]
    context_rows = text_kv.shape[2]
    self_heads, text_heads = HEADS // count, HEADS // half
    self_span, text_span = self_heads * HEAD_DIM, text_heads * HEAD_DIM

    def swap(tensor, step):
        return lax.ppermute(tensor, "seq", [(i, i ^ step) for i in range(count)])

    bf16 = jnp.bfloat16
    text_blocks = pl.pallas_call(
        functools.partial(pack_text_kernel, half),
        out_shape=[jax.ShapeDtypeStruct((2, context_rows, text_span), bf16)] * half,
        in_specs=[HBM_SPEC],
        out_specs=[VMEM_SPEC] * half,
        scratch_shapes=[pltpu.SemaphoreType.DMA((half,))],
        compiler_params=pltpu.CompilerParams(vmem_limit_bytes=4 << 20),
        name="pack_text",
    )(text_kv)
    row_blocks = pl.pallas_call(
        functools.partial(pack_rows_kernel, count, self_span, text_span),
        out_shape=[jax.ShapeDtypeStruct((rows, 3 * self_span + text_span), bf16)] * count,
        in_specs=[HBM_SPEC] * 4,
        out_specs=[VMEM_SPEC] * count,
        scratch_shapes=[pltpu.SemaphoreType.DMA((count, 4))],
        compiler_params=pltpu.CompilerParams(vmem_limit_bytes=4 << 20),
        name="pack_rows",
    )(self_queries, self_keys, self_values, text_queries)
    near = [swap(text_blocks[s], s) for s in range(half - 1, 0, -1)] + [text_blocks[0]]
    arrived = [swap(row_blocks[s], s) for s in range(count - 1, 0, -1)] + [row_blocks[0]]
    mixed = pl.pallas_call(
        functools.partial(attend_kernel, count, self_heads, text_heads),
        out_shape=[jax.ShapeDtypeStruct((rows, self_span + text_span + LANES), bf16)] * count,
        in_specs=[SMEM_SPEC] + [VMEM_SPEC] * (count + half),
        out_specs=[VMEM_SPEC] * count,
        compiler_params=pltpu.CompilerParams(vmem_limit_bytes=16 << 20),
        name="attend",
    )(text_len, *near, *arrived)
    returned = [swap(mixed[s], s) for s in range(count - 1, 0, -1)] + [mixed[0]]
    shape = jax.ShapeDtypeStruct((1, rows, channels), bf16)
    return tuple(
        pl.pallas_call(
            functools.partial(combine_kernel, count, self_heads, text_heads),
            out_shape=[shape, shape],
            in_specs=[VMEM_SPEC] * count,
            out_specs=[VMEM_SPEC] * 2,
            compiler_params=pltpu.CompilerParams(vmem_limit_bytes=4 << 20),
        name="combine",
        )(*returned)
    )


def shards(*arrays):
    count = lax.axis_size("seq")
    power_of_two = count > 1 and count & (count - 1) == 0
    if power_of_two and HEADS % count == 0 and 6 * (2 * HEADS // count) <= LANES:
        return halves_shards(*arrays)
    return general_shards(*arrays)


def solution(mesh):
    return jax.shard_map(
        shards,
        mesh=mesh,
        in_specs=(
            P("enc", ("groups", "seq"), None),
            P("enc", ("groups", "seq"), None),
            P("enc", ("groups", "seq"), None),
            P("enc", ("groups", "seq"), None),
            P("enc", None, ("groups", "seq"), None),
            P("groups"),
        ),
        out_specs=(P("enc", ("groups", "seq"), None), P("enc", ("groups", "seq"), None)),
        check_vma=False,
    )
```

```python
import functools
import math

import jax
import jax.numpy as jnp
from jax import lax
from jax.experimental import pallas as pl
from jax.experimental.pallas import tpu as pltpu
from jax.sharding import PartitionSpec as P

HEADS = 32
HEAD_DIM = 128
LANES = 128


def absorb(run_state, queries, key_rows, value_rows, live_mask):
    running_max, row_total, weighted_sum = run_state
    scores = jnp.einsum(
        "qpd,kpd->pqk", queries, key_rows, preferred_element_type=jnp.float32
    ) / math.sqrt(HEAD_DIM)
    scores = jnp.where(live_mask[None, None, :], scores, -1e30)
    new_max = jnp.maximum(running_max, jnp.max(scores, axis=2))
    weights = jnp.where(live_mask[None, None, :], jnp.exp(scores - new_max[:, :, None]), 0.0)
    factor = jnp.exp(running_max - new_max)
    row_total = row_total * factor + jnp.sum(weights, axis=2)
    weighted_sum = weighted_sum * factor[:, :, None] + jnp.einsum(
        "pqk,kpd->pqd", weights.astype(jnp.bfloat16), value_rows, preferred_element_type=jnp.float32
    )
    return (new_max, row_total, weighted_sum)


def empty_state(head_count, query_count):
    return (
        jnp.full((head_count, query_count), -1e30, jnp.float32),
        jnp.zeros((head_count, query_count), jnp.float32),
        jnp.zeros((head_count, query_count, HEAD_DIM), jnp.float32),
    )


def finish(run_state):
    running_max, row_total, weighted_sum = run_state
    return (weighted_sum / row_total[:, :, None]).transpose(1, 0, 2).astype(jnp.bfloat16)


def block_attention(queries, key_rows, value_rows, live_mask):
    query_total, heads_here, head_width = queries.shape
    key_total = key_rows.shape[0]
    key_block = 1024 if key_total % 1024 == 0 else key_total
    query_block = 512 if query_total % 512 == 0 else query_total
    key_blocks = key_rows.reshape(key_total // key_block, key_block, heads_here, head_width)
    value_blocks = value_rows.reshape(key_total // key_block, key_block, heads_here, head_width)
    live_blocks = live_mask.reshape(key_total // key_block, key_block)

    def one_block(query_piece):

        def absorb_block(run_state, pieces):
            return (absorb(run_state, query_piece, pieces[0], pieces[1], pieces[2]), None)

        final_state, unused = lax.scan(
            absorb_block,
            empty_state(heads_here, query_block),
            (key_blocks, value_blocks, live_blocks),
        )
        return finish(final_state)

    blended = lax.map(
        one_block, queries.reshape(query_total // query_block, query_block, heads_here, head_width)
    )
    return blended.reshape(query_total, heads_here, head_width)


def general_shards(self_queries, self_keys, self_values, text_queries, text_kv, text_len):
    token_rows = self_queries.shape[1]
    channel_count = self_queries.shape[2]
    seq_count = lax.axis_size("seq")
    quarter_count = max(seq_count // HEADS, 1)
    heads_here = max(HEADS // seq_count, 1)
    group_count = HEADS // heads_here
    head_span = heads_here * HEAD_DIM
    share_rows = token_rows // quarter_count
    query_total = share_rows * seq_count
    branch = lax.axis_index("enc")
    length = lax.dynamic_index_in_dim(text_len, branch, 0, keepdims=False)

    def head_view(tensor):
        return tensor.reshape(1, share_rows, seq_count, head_span)

    def repeated(tensor):
        spread = jnp.broadcast_to(
            tensor.reshape(1, token_rows, 1, group_count, head_span),
            (1, token_rows, quarter_count, group_count, head_span),
        )
        return spread.reshape(1, token_rows, seq_count, head_span)

    head_queries, head_keys, head_values = (
        lax.all_to_all(head_view(self_queries), "seq", split_axis=2, concat_axis=1, tiled=True),
        lax.all_to_all(repeated(self_keys), "seq", split_axis=2, concat_axis=1, tiled=True),
        lax.all_to_all(repeated(self_values), "seq", split_axis=2, concat_axis=1, tiled=True),
    )
    key_rows = head_keys.reshape(-1, heads_here, HEAD_DIM)
    value_rows = head_values.reshape(-1, heads_here, HEAD_DIM)
    query_rows = head_queries.reshape(query_total, heads_here, HEAD_DIM)
    every_key = jnp.ones((key_rows.shape[0],), jnp.bool_)
    self_heads = block_attention(query_rows, key_rows, value_rows, every_key)
    head_text_queries = lax.all_to_all(
        head_view(text_queries), "seq", split_axis=2, concat_axis=1, tiled=True
    )
    context_rows = text_kv.shape[2]
    spread = jnp.broadcast_to(
        text_kv.reshape(1, 2, context_rows, 1, group_count, head_span),
        (1, 2, context_rows, quarter_count, group_count, head_span),
    )
    head_context = lax.all_to_all(
        spread.reshape(1, 2, context_rows, seq_count, head_span),
        "seq",
        split_axis=3,
        concat_axis=2,
        tiled=True,
    )
    text_total = head_context.shape[2]
    context_keys = head_context[0, 0].reshape(text_total, heads_here, HEAD_DIM)
    context_values = head_context[0, 1].reshape(text_total, heads_here, HEAD_DIM)
    live_mask = jnp.arange(text_total, dtype=jnp.int32) < length
    text_heads = block_attention(
        head_text_queries.reshape(query_total, heads_here, HEAD_DIM),
        context_keys,
        context_values,
        live_mask,
    )
    self_view = self_heads.reshape(1, seq_count, share_rows, 1, head_span)
    text_view = text_heads.reshape(1, seq_count, share_rows, 1, head_span)
    self_back, text_back = (
        lax.all_to_all(self_view, "seq", split_axis=1, concat_axis=3, tiled=True),
        lax.all_to_all(text_view, "seq", split_axis=1, concat_axis=3, tiled=True),
    )
    self_mixed = self_back.reshape(1, token_rows, channel_count)
    text_mixed = text_back.reshape(1, token_rows, channel_count)
    return (self_mixed, text_mixed)


VMEM_SPEC = pl.BlockSpec(memory_space=pltpu.VMEM)
HBM_SPEC = pl.BlockSpec(memory_space=pltpu.HBM)


def columns(index, width):
    return pl.ds(pl.multiple_of(index * width, width), width)


def run_copies(copies):
    for copy in copies:
        copy.start()
    for copy in copies:
        copy.wait()


def pack_text_kernel(half, steps, text_ref, *refs):
    out_refs, sems = refs[:-1], refs[-1]
    me = lax.axis_index("seq")
    width = out_refs[0].shape[2]
    run_copies(
        [
            pltpu.make_async_copy(
                text_ref.at[0, :, :, columns(lax.rem(me ^ step, half), width)], out_ref, sems.at[place]
            )
            for place, (step, out_ref) in enumerate(zip(steps, out_refs))
        ]
    )


def pack_rows_kernel(count, self_span, text_span, q_ref, k_ref, v_ref, t_ref, length_ref, *refs):
    out_refs, bias_ref, sems, length_smem, length_sem = refs[:count], *refs[count:]
    half = count // 2
    me = lax.axis_index("seq")
    copies = [pltpu.make_async_copy(length_ref, length_smem, length_sem)]
    for step in range(count):
        other = me ^ step
        for place, source in enumerate((q_ref, k_ref, v_ref)):
            copies.append(
                pltpu.make_async_copy(
                    source.at[0, :, columns(other, self_span)],
                    out_refs[step].at[:, pl.ds(place * self_span, self_span)],
                    sems.at[step, place],
                )
            )
        copies.append(
            pltpu.make_async_copy(
                t_ref.at[0, :, columns(lax.rem(other, half), text_span)],
                out_refs[step].at[:, pl.ds(3 * self_span, text_span)],
                sems.at[step, 3],
            )
        )
    run_copies(copies)
    length = length_smem[lax.axis_index("enc")]
    context_rows = bias_ref.shape[1] // half
    spots = lax.broadcasted_iota(jnp.int32, (8, half * context_rows), 1)
    block = lax.div(spots, context_rows)
    position = (me ^ block) * context_rows + (spots - block * context_rows)
    bias_ref[0:8] = jnp.where(position < length, 0.0, -1e30)
    start = lax.div(me, half) * (half * context_rows)
    bias_ref[8:16] = jnp.where(spots * 0 + start < length, 1.0, 0.0)


def matmul_nt(a, b):
    return lax.dot_general(a, b, (((1,), (1,)), ((), ())), preferred_element_type=jnp.float32)


def gathered(refs, start):
    return jnp.concatenate([ref[:, pl.ds(start, HEAD_DIM)] for ref in refs], axis=0)


def scatter(refs, start, values):
    rows = values.shape[0] // len(refs)
    for step, ref in enumerate(refs):
        ref[:, pl.ds(start, values.shape[1])] = values[step * rows : (step + 1) * rows]


def self_kernel(count, self_heads, *refs):
    row_refs, out_refs = refs[:count][::-1], refs[count:]
    self_span = self_heads * HEAD_DIM
    for head in range(self_heads):
        at = head * HEAD_DIM
        queries, keys, values = (gathered(row_refs, place * self_span + at) for place in range(3))
        scores = matmul_nt(queries, keys) * (1.0 / math.sqrt(HEAD_DIM))
        weights = jnp.exp(scores - jnp.max(scores, axis=1, keepdims=True))
        row_sum = jnp.sum(weights, axis=1, keepdims=True)
        mixed = jnp.dot(weights.astype(jnp.bfloat16), values, preferred_element_type=jnp.float32)
        scatter(out_refs, at, (mixed / row_sum).astype(jnp.bfloat16))


def text_kernel(count, self_heads, text_heads, bias_ref, *refs):
    half = count // 2
    text_refs, row_refs = refs[:half][::-1], refs[half : half + count][::-1]
    out_refs = refs[half + 2 * count :]
    self_span, text_span = self_heads * HEAD_DIM, text_heads * HEAD_DIM
    total = row_refs[0].shape[0] * count
    scale = 1.0 / math.sqrt(HEAD_DIM)
    dead_bias = bias_ref[0:1, :]
    any_live = bias_ref[8:9, 0:1]
    lane = lax.broadcasted_iota(jnp.int32, (total, LANES), 1)
    stats = jnp.zeros((total, LANES), jnp.float32)
    for head in range(text_heads):
        at = head * HEAD_DIM
        queries = gathered(row_refs, 3 * self_span + at)
        keys = jnp.concatenate([ref[0, :, pl.ds(at, HEAD_DIM)] for ref in text_refs], axis=0)
        values = jnp.concatenate([ref[1, :, pl.ds(at, HEAD_DIM)] for ref in text_refs], axis=0)
        scores = matmul_nt(queries, keys) * scale + dead_bias
        top = jnp.max(scores, axis=1, keepdims=True)
        weights = jnp.exp(scores - top)
        row_sum = jnp.sum(weights, axis=1, keepdims=True)
        mixed = jnp.dot(weights.astype(jnp.bfloat16), values, preferred_element_type=jnp.float32)
        scatter(out_refs, self_span + at, (mixed / row_sum).astype(jnp.bfloat16))
        stats = jnp.where(lane == head, top, stats)
        stats = jnp.where(lane == text_heads + head, row_sum * any_live, stats)
    high = stats.astype(jnp.bfloat16).astype(jnp.float32)
    rest = stats - high
    middle = rest.astype(jnp.bfloat16).astype(jnp.float32)
    low = rest - middle
    stride = 2 * text_heads
    pieces = high + pltpu.roll(middle, stride, 1) + pltpu.roll(low, 2 * stride, 1)
    scatter(out_refs, self_span + text_span, pieces.astype(jnp.bfloat16))


def combine_kernel(count, self_heads, text_heads, *refs):
    half = count // 2
    in_refs, (self_ref, text_ref) = refs[:count][::-1], refs[count:]
    self_span, text_span = self_heads * HEAD_DIM, text_heads * HEAD_DIM
    me = lax.axis_index("seq")
    stride = 2 * text_heads

    def read_stats(ref):
        pieces = ref[:, pl.ds(self_span + text_span, LANES)].astype(jnp.float32)
        stats = pieces + (
            pltpu.roll(pieces, LANES - stride, 1) + pltpu.roll(pieces, LANES - 2 * stride, 1)
        )
        return stats, pltpu.roll(stats, LANES - text_heads, 1)

    for step in range(count):
        self_ref[0, :, columns(me ^ step, self_span)] = in_refs[step][:, pl.ds(0, self_span)]
    for step in range(half):
        near, far = in_refs[step], in_refs[step ^ half]
        near_top, near_sum = read_stats(near)
        far_top, far_sum = read_stats(far)
        top = jnp.maximum(near_top, far_top)
        near_part = near_sum * jnp.exp(near_top - top)
        far_part = far_sum * jnp.exp(far_top - top)
        both = near_part + far_part
        near_share, far_share = near_part / both, far_part / both
        group = lax.rem(me ^ step, half)
        for head in range(text_heads):
            at = self_span + head * HEAD_DIM
            mixed = near[:, pl.ds(at, HEAD_DIM)].astype(jnp.float32) * near_share[:, head : head + 1]
            mixed += far[:, pl.ds(at, HEAD_DIM)].astype(jnp.float32) * far_share[:, head : head + 1]
            text_ref[0, :, columns(group * text_heads + head, HEAD_DIM)] = mixed.astype(jnp.bfloat16)


def halves_shards(self_queries, self_keys, self_values, text_queries, text_kv, text_len):
    count = lax.axis_size("seq")
    half = count // 2
    rows, channels = self_queries.shape[1], self_queries.shape[2]
    context_rows = text_kv.shape[2]
    self_heads, text_heads = HEADS // count, HEADS // half
    self_span, text_span = self_heads * HEAD_DIM, text_heads * HEAD_DIM

    def swap(tensor, step):
        return lax.ppermute(tensor, "seq", [(i, i ^ step) for i in range(count)])

    bf16 = jnp.bfloat16

    def pack_text(steps):
        return pl.pallas_call(
            functools.partial(pack_text_kernel, half, steps),
            out_shape=[jax.ShapeDtypeStruct((2, context_rows, text_span), bf16)] * len(steps),
            in_specs=[HBM_SPEC],
            out_specs=[VMEM_SPEC] * len(steps),
            scratch_shapes=[pltpu.SemaphoreType.DMA((len(steps),))],
            compiler_params=pltpu.CompilerParams(vmem_limit_bytes=4 << 20),
            name="pack_text",
        )(pltpu.with_memory_space_constraint(text_kv, pltpu.HBM))

    first = max(half // 2, 1)
    later = [step for step in range(half) if step != first]
    text_blocks = {first: pack_text([first])[0]} if half > 1 else {}
    text_blocks.update(zip(later, pack_text(later)))
    *row_blocks, bias = pl.pallas_call(
        functools.partial(pack_rows_kernel, count, self_span, text_span),
        out_shape=[jax.ShapeDtypeStruct((rows, 3 * self_span + text_span), bf16)] * count
        + [jax.ShapeDtypeStruct((16, half * context_rows), jnp.float32)],
        in_specs=[HBM_SPEC] * 5,
        out_specs=[VMEM_SPEC] * (count + 1),
        scratch_shapes=[
            pltpu.SemaphoreType.DMA((count, 4)),
            pltpu.SMEM(text_len.shape, jnp.int32),
            pltpu.SemaphoreType.DMA,
        ],
        compiler_params=pltpu.CompilerParams(vmem_limit_bytes=4 << 20),
        name="pack_rows",
    )(self_queries, self_keys, self_values, text_queries, text_len)
    near = {step: swap(block, step) if step else block for step, block in text_blocks.items()}
    arrived = [swap(row_blocks[s], s) for s in range(count - 1, 0, -1)] + [row_blocks[0]]
    out_block = jax.ShapeDtypeStruct((rows, self_span + text_span + LANES), bf16)
    mixed = pl.pallas_call(
        functools.partial(self_kernel, count, self_heads),
        out_shape=[out_block] * count,
        in_specs=[VMEM_SPEC] * count,
        out_specs=[VMEM_SPEC] * count,
        compiler_params=pltpu.CompilerParams(vmem_limit_bytes=8 << 20),
        name="self_attend",
    )(*arrived)
    mixed = pl.pallas_call(
        functools.partial(text_kernel, count, self_heads, text_heads),
        out_shape=[out_block] * count,
        in_specs=[VMEM_SPEC] * (1 + 2 * count + half),
        out_specs=[VMEM_SPEC] * count,
        input_output_aliases={1 + half + count + i: i for i in range(count)},
        compiler_params=pltpu.CompilerParams(vmem_limit_bytes=16 << 20),
        name="text_attend",
    )(bias, *[near[step] for step in range(half - 1, -1, -1)], *arrived, *mixed)
    returned = [swap(mixed[s], s) for s in range(count - 1, 0, -1)] + [mixed[0]]
    shape = jax.ShapeDtypeStruct((1, rows, channels), bf16)
    return tuple(
        pl.pallas_call(
            functools.partial(combine_kernel, count, self_heads, text_heads),
            out_shape=[shape, shape],
            in_specs=[VMEM_SPEC] * count,
            out_specs=[VMEM_SPEC] * 2,
            compiler_params=pltpu.CompilerParams(vmem_limit_bytes=4 << 20),
        name="combine",
        )(*returned)
    )


def shards(*arrays):
    count = lax.axis_size("seq")
    power_of_two = count > 1 and count & (count - 1) == 0
    if power_of_two and HEADS % count == 0 and 6 * (2 * HEADS // count) <= LANES:
        return halves_shards(*arrays)
    return general_shards(*arrays)


def solution(mesh):
    return jax.shard_map(
        shards,
        mesh=mesh,
        in_specs=(
            P("enc", ("groups", "seq"), None),
            P("enc", ("groups", "seq"), None),
            P("enc", ("groups", "seq"), None),
            P("enc", ("groups", "seq"), None),
            P("enc", None, ("groups", "seq"), None),
            P("groups"),
        ),
        out_specs=(P("enc", ("groups", "seq"), None), P("enc", ("groups", "seq"), None)),
        check_vma=False,
    )
```
